32 devices in a mesh: groups: 2 (over x), ctx: 16 (over z, y, core).
Axes of the slice: x: 2, y: 2, z: 4, core: 2. Of those that a mesh axis runs over, the one named last changes fastest.
Arguments:
- hidden_in: bfloat16 [4096, 2048], P(('groups', 'ctx')), parts along dimension 0, may hold values from -6 to 6
- queries: bfloat16 [4096, 1024], P(('groups', 'ctx')), parts along dimension 0, as said below
- keys: bfloat16 [4096, 128], P(('groups', 'ctx')), parts along dimension 0, as said below
- values: bfloat16 [4096, 128], P(('groups', 'ctx')), parts along dimension 0, may hold values from -6 to 6
- out_weight: bfloat16 [1024, 2048], replicated, may hold values from -0.5 to 0.5
- norm_gain: float32 [2048], replicated, may hold values from 0.1 to 1.9
- gate_weight: bfloat16 [2048, 11008], P(None, 'ctx'), may hold values from -0.125 to 0.125
- up_weight: bfloat16 [2048, 11008], P(None, 'ctx'), may hold values from -0.125 to 0.125
- down_weight: bfloat16 [11008, 2048], P('ctx'), may hold values from -0.0546875 to 0.0546875
- pair_ids: int32 [4096], P('groups'), parts along dimension 0, may hold values from 0 to 3, as said below
- roles: int32 [4096], P('groups'), parts along dimension 0, may hold values from 0 to 2, as said below
- send_rows: int32 [32, 128], P(('groups', 'ctx')), parts along dimension 0, may hold values from 0 to 127, as said below
- send_counts: int32 [32, 16], P('groups'), parts along dimension 0, may hold values from 0 to 8, as said below
Outputs:
- layer_out: bfloat16 [4096, 2048], P(('groups', 'ctx')), parts along dimension 0
The draws below stay inside these ranges and needn't reach their ends.
There are 2 independent parts, one for each index of `groups`. The reference program is written for one: setup_inputs(seed, part) draws one part's arguments, and reference() takes and returns one part's arrays. A program takes and returns all parts, laid end to end along the dimension named above; an argument that names none is the same for every part. Nothing has to cross between parts.
Inputs may be any that keep to these rules, and one draw needn't show every extreme that they name: `pair_ids`: never falls along the sequence; every pair is present, and one pair's chosen response spans 256 positions or more. `roles`: each pair is a prompt, then its chosen response, then its rejected response, each of one position or more; responses fill exactly 1536 positions. `send_rows`: slots j * 8 + k with k < send_counts[i, j] list distinct local rows of device i, together exactly its positions whose role is not 0; other slots hold 0. `send_counts`: replicated on every device; every column sums to 96; some entry equals 8. `queries`: values within -8 to 8. `keys`: values within -8 to 8.
All inputs are finite; a program needn't handle non-finite values.
Results may differ from the reference program's by a relative error of at most 0.015.
Values may be sent and summed in bfloat16 or wider, within the bound.
A program may use at most 128 MiB of HBM per device.

```python
import math
import jax
import jax.numpy as jnp
from jax import lax

D = 2048
FF = 11008
QH = 8
HD = 128
TOK_DEV = 128
SEQ = 2048
LIVE_DEV = 96
CAP = 8
PAIRS = 4
N_CTX = 16


def structure(key):
    base_key = jax.random.fold_in(key, 31)
    key_a, key_b, key_c, key_d = jax.random.split(base_key, 4)
    live_total = LIVE_DEV * N_CTX
    prompt_total = SEQ - live_total
    zero_one = jnp.zeros((1,), jnp.int32)
    first_prompt = jax.random.randint(key_c, (), 1, TOK_DEV + 1, dtype=jnp.int32)
    extra_len = jax.random.randint(key_d, (), 0, TOK_DEV // 2, dtype=jnp.int32)
    first_chosen = N_CTX // 2 * TOK_DEV - first_prompt + extra_len
    prompt_static = prompt_total - TOK_DEV
    prompt_cuts = jnp.sort(jax.random.permutation(key_a, prompt_static - 1)[:PAIRS - 2].astype(jnp.int32) + 1)
    prompt_edges = jnp.concatenate([zero_one, prompt_cuts, jnp.full((1,), prompt_static, jnp.int32)])
    prompt_pieces = prompt_edges[1:] - prompt_edges[:-1]
    prompt_pieces = prompt_pieces.at[-1].add(TOK_DEV - first_prompt)
    answer_static = live_total - N_CTX // 2 * TOK_DEV - TOK_DEV // 2
    answer_cuts = jnp.sort(jax.random.permutation(key_b, answer_static - 1)[:2 * PAIRS - 2].astype(jnp.int32) + 1)
    answer_edges = jnp.concatenate([zero_one, answer_cuts, jnp.full((1,), answer_static, jnp.int32)])
    answers = answer_edges[1:] - answer_edges[:-1]
    prompts = jnp.concatenate([first_prompt[None], prompt_pieces])
    chosen = jnp.concatenate([first_chosen[None], answers[1::2]])
    rejected = jnp.concatenate([(answers[0] + first_prompt - extra_len + TOK_DEV // 2)[None], answers[2::2]])
    lengths = jnp.stack([prompts, chosen, rejected], axis=1).reshape(-1)
    piece_ends = jnp.cumsum(lengths).astype(jnp.int32)
    positions = jnp.arange(SEQ, dtype=jnp.int32)
    piece_of = jnp.sum((positions[:, None] >= piece_ends[None, :]).astype(jnp.int32), axis=1)
    pair_of = piece_of // 3
    role_of = piece_of % 3
    live_flag = (role_of != 0).astype(jnp.int32)
    live_rank = (jnp.cumsum(live_flag) - live_flag).astype(jnp.int32)
    device_of = positions // TOK_DEV
    first_rank = live_rank[device_of * TOK_DEV]
    target_dev = live_rank % N_CTX
    slot_index = (live_rank - first_rank) // N_CTX
    flat_slot = jnp.where(live_flag == 1, device_of * (N_CTX * CAP) + target_dev * CAP + slot_index, N_CTX * N_CTX * CAP)
    send_table = jnp.zeros((N_CTX * N_CTX * CAP,), jnp.int32).at[flat_slot].set(positions % TOK_DEV, mode='drop')
    count_slot = jnp.where(live_flag == 1, device_of * N_CTX + target_dev, N_CTX * N_CTX)
    count_table = jnp.zeros((N_CTX * N_CTX,), jnp.int32).at[count_slot].add(1, mode='drop')
    return (pair_of, role_of, send_table.reshape(N_CTX, N_CTX * CAP), count_table.reshape(N_CTX, N_CTX))


def draw_pair_ids(key, part):
    return structure(key)[0]


def draw_roles(key, part):
    return structure(key)[1]


def draw_send_rows(key, part):
    return structure(key)[2]


def draw_send_counts(key, part):
    return structure(key)[3]


def draw_queries(key, part):
    base_draw = jnp.clip(jax.random.normal(jax.random.fold_in(key, 5), (SEQ, QH * HD), jnp.float32), -4.0, 4.0)
    return base_draw.astype(jnp.bfloat16)


def draw_keys(key, part):
    base_draw = jnp.clip(jax.random.normal(jax.random.fold_in(key, 6), (SEQ, HD), jnp.float32), -4.0, 4.0)
    return base_draw.astype(jnp.bfloat16)


def levels(own_key, shape, shards, least, top_value):
    def one(position, parts):
        steps = jax.random.uniform(jax.random.fold_in(jax.random.fold_in(own_key, 6), position), (parts,), jnp.float32, least / len(shards), top_value / len(shards))
        return jnp.repeat(jnp.exp(steps), shape[position] // parts).reshape((-1,) + (1,) * (len(shape) - position - 1))

    gain = one(*shards[0])
    for cut in shards[1:]:
        gain = gain * one(*cut)
    return gain


def noise(own_key, shape, scale, most, pieces=(), kind=jnp.bfloat16):
    values = scale * jax.random.normal(own_key, shape, jnp.float32)
    if pieces:
        values = values * levels(own_key, shape, pieces, -0.22, 0.18)
    return jnp.clip(values, -most, most).astype(kind)


def setup_inputs(seed: int = 0, part: int = 0) -> dict:
    streams_of = jax.random.split(jax.random.key(seed), 14)
    part_splits = jax.random.split(jax.random.fold_in(streams_of[13], part), 14)
    return {
        "hidden_in": noise(part_splits[0], (SEQ, D), 1.0, 6.0, ((0, 16),)),
        "queries": draw_queries(jax.random.fold_in(jax.random.fold_in(streams_of[13], part), 71), part),
        "keys": draw_keys(jax.random.fold_in(jax.random.fold_in(streams_of[13], part), 71), part),
        "values": noise(part_splits[3], (SEQ, HD), 1.0, 6.0, ((0, 16),)),
        "out_weight": noise(streams_of[4], (QH * HD, D), HD ** -0.5, 0.5),
        "norm_gain": jnp.clip(1.0 + 0.18 * jax.random.normal(streams_of[5], (D,), jnp.float32), 0.1, 1.9),
        "gate_weight": noise(streams_of[6], (D, FF), D ** -0.5, 0.125, ((1, 16),)),
        "up_weight": noise(streams_of[7], (D, FF), D ** -0.5, 0.125, ((1, 16),)),
        "down_weight": noise(streams_of[8], (FF, D), FF ** -0.5, 0.0546875, ((0, 16),)),
        "pair_ids": draw_pair_ids(jax.random.fold_in(jax.random.fold_in(streams_of[13], part), 71), part),
        "roles": draw_roles(jax.random.fold_in(jax.random.fold_in(streams_of[13], part), 71), part),
        "send_rows": draw_send_rows(jax.random.fold_in(jax.random.fold_in(streams_of[13], part), 71), part),
        "send_counts": draw_send_counts(jax.random.fold_in(jax.random.fold_in(streams_of[13], part), 71), part),
    }


NEG_FILL = -1e+30

def reference(hidden_in, queries, keys, values, out_weight, norm_gain, gate_weight, up_weight, down_weight, pair_ids, roles, send_rows, send_counts):
    seq_len = hidden_in.shape[0]
    head_count = queries.shape[1] // HD
    block_rows = math.gcd(seq_len, 512)
    query_heads = queries.reshape(seq_len, head_count, HD).astype(jnp.float32)
    key_all = keys.astype(jnp.float32)
    value_all = values.astype(jnp.float32)
    key_pos = jnp.arange(seq_len, dtype=jnp.int32)
    score_scale = 1.0 / math.sqrt(HD)

    def attend(block_index):
        begin_row = (block_index * block_rows).astype(jnp.int32)
        query_block = lax.dynamic_slice_in_dim(query_heads, begin_row, block_rows)
        query_pos = begin_row + jnp.arange(block_rows, dtype=jnp.int32)
        query_pair = lax.dynamic_slice_in_dim(pair_ids, begin_row, block_rows)
        query_role = lax.dynamic_slice_in_dim(roles, begin_row, block_rows)
        seen_mask = (query_pair[:, None] == pair_ids[None, :]) & (key_pos[None, :] <= query_pos[:, None]) & ((roles[None, :] == 0) | (roles[None, :] == query_role[:, None]))
        scores = jnp.einsum('tqd,kd->qtk', query_block, key_all) * score_scale
        masked = jnp.where(seen_mask[None], scores, NEG_FILL)
        maximum = lax.optimization_barrier(jnp.max(masked, axis=-1, keepdims=True))
        weights = jnp.where(seen_mask[None], jnp.exp(masked - maximum), 0.0)
        denominator = lax.optimization_barrier(jnp.sum(weights, axis=-1))
        rounded = lax.optimization_barrier(weights.astype(jnp.bfloat16)).astype(jnp.float32)
        numerator = jnp.einsum('qtk,kd->qtd', rounded, value_all)
        mixed_sum = numerator / denominator[..., None]
        return mixed_sum.transpose(1, 0, 2).reshape(block_rows, head_count * HD)
    attention = lax.map(attend, jnp.arange(seq_len // block_rows, dtype=jnp.int32))
    attention = attention.reshape(seq_len, head_count * HD).astype(jnp.bfloat16)
    residual = (hidden_in.astype(jnp.float32) + jnp.dot(attention, out_weight, preferred_element_type=jnp.float32)).astype(jnp.bfloat16)
    wide = residual.astype(jnp.float32)
    mean_sq = lax.optimization_barrier(jnp.mean(wide * wide, axis=-1, keepdims=True))
    normed = (wide * lax.rsqrt(mean_sq + 1e-06) * norm_gain.astype(jnp.float32)[None, :]).astype(jnp.bfloat16)
    capacity = send_rows.shape[1] // N_CTX
    slot_index = jnp.arange(N_CTX * capacity, dtype=jnp.int32)
    valid = (slot_index % capacity)[None, :] < jnp.repeat(send_counts, capacity, axis=1)
    owner = jnp.arange(N_CTX, dtype=jnp.int32)[:, None] * TOK_DEV + send_rows
    target = jnp.where(valid, owner, seq_len).reshape(-1)
    live_mask = jnp.zeros((seq_len,), jnp.float32).at[target].set(1.0, mode='drop')
    ff_dev = FF // N_CTX

    def add_term(carry, shard_index):
        begin_col = (shard_index * ff_dev).astype(jnp.int32)
        gate_slice = lax.dynamic_slice_in_dim(gate_weight, begin_col, ff_dev, 1)
        up_slice = lax.dynamic_slice_in_dim(up_weight, begin_col, ff_dev, 1)
        down_slice = lax.dynamic_slice_in_dim(down_weight, begin_col, ff_dev, 0)
        gate_out = jnp.dot(normed, gate_slice, preferred_element_type=jnp.float32)
        up_out = jnp.dot(normed, up_slice, preferred_element_type=jnp.float32)
        inner_out = (jax.nn.silu(gate_out) * up_out).astype(jnp.bfloat16)
        term_out = jnp.dot(inner_out, down_slice, preferred_element_type=jnp.float32).astype(jnp.bfloat16)
        term_out = lax.optimization_barrier(term_out)
        return (carry + term_out.astype(jnp.float32), None)
    ffn_sum, _ = lax.scan(add_term, jnp.zeros((seq_len, hidden_in.shape[1]), jnp.float32), jnp.arange(N_CTX, dtype=jnp.int32))
    ffn_round = lax.optimization_barrier(ffn_sum.astype(jnp.bfloat16)).astype(jnp.float32)
    return (residual.astype(jnp.float32) + live_mask[:, None] * ffn_round).astype(jnp.bfloat16)
```

```python
import functools

import jax
import jax.numpy as jnp
from jax import lax
from jax.experimental import pallas as pl
from jax.experimental.pallas import tpu as pltpu
from jax.sharding import PartitionSpec as P

NEG_FILL = -1e30
MESH = pl.DeviceIdType.MESH
PLANES = 2
CORES = 2
DOWN_TILE = 512


def place(n):
    me = lax.axis_index("ctx")
    return me, me // (PLANES * CORES), (me // CORES) % PLANES, me % CORES


def index_of(z, y, c):
    return (z * PLANES + y) * CORES + c


def near_first(z, i, stages):
    short = jnp.minimum(z, stages - 1 - z)
    step = (i + 1) // 2
    inner = jnp.where(i % 2 == 1, z + step, z - step)
    outer = jnp.where(z < stages - 1 - z, z + i - short, z - i + short)
    return jnp.where(i <= 2 * short, inner, outer)


def greet(n):
    me, z, y, c = place(n)
    stages = n // (PLANES * CORES)
    barrier = pltpu.get_barrier_semaphore()

    def hello(target):
        pl.semaphore_signal(barrier, inc=1, device_id={"ctx": target}, device_id_type=MESH)

    hello(index_of(z, 1 - y, c))
    hello(index_of(z, y, 1 - c))
    pl.when(z > 0)(lambda: hello(index_of(z - 1, y, c)))
    pl.when(z < stages - 1)(lambda: hello(index_of(z + 1, y, c)))
    pl.semaphore_wait(barrier, 2 + (z > 0).astype(jnp.int32) + (z < stages - 1).astype(jnp.int32))


def remote(src, dst, send_sem, recv_sem, target):
    return pltpu.make_async_remote_copy(
        src_ref=src,
        dst_ref=dst,
        send_sem=send_sem,
        recv_sem=recv_sem,
        device_id={"ctx": target},
        device_id_type=MESH,
    )


class Spread:
    def __init__(self, n, rows, full, send, recv):
        self.n, self.rows, self.full, self.send, self.recv = n, rows, full, send, recv
        self.me, self.z, self.y, self.c = place(n)
        self.stages = n // (PLANES * CORES)

    def block(self, b):
        return self.full.at[pl.ds(pl.multiple_of(b * self.rows, self.rows), self.rows)]

    def copy(self, b, way, target):
        return remote(
            self.block(b), self.block(b), self.send.at[b, way], self.recv.at[b], target
        )

    def wait_for(self, b):
        self.copy(b, 0, index_of(self.z, self.y, 1 - self.c)).wait_recv()

    def ways(self, i, act):
        z, y, c = self.z, self.y, self.c
        far = near_first(z, i, self.stages)
        b = index_of(far, y, c)
        act(self.copy(b, 0, index_of(z, 1 - y, c)))
        pl.when((z < self.stages - 1) & (far <= z))(
            lambda: act(self.copy(b, 1, index_of(z + 1, y, c)))
        )
        pl.when((z > 0) & (far >= z))(lambda: act(self.copy(b, 2, index_of(z - 1, y, c))))
        act(self.copy(b, 3, index_of(z, y, 1 - c)))

    def start_own(self, i):
        pl.when(i > 0)(
            lambda: self.wait_for(index_of(near_first(self.z, i, self.stages), self.y, self.c))
        )
        self.ways(i, lambda copy: copy.start())

    def cross(self, i):
        b = index_of(near_first(self.z, i, self.stages), 1 - self.y, self.c)
        return b, self.copy(b, 3, index_of(self.z, self.y, 1 - self.c))

    def start_cross(self, i):
        b, copy = self.cross(i)
        self.wait_for(b)
        copy.start()

    def finish(self):
        def body(i, carry):
            self.ways(i, lambda copy: copy.wait_send())
            self.cross(i)[1].wait_send()
            return carry

        lax.fori_loop(0, self.stages, body, 0)


def gather_kernel(n, x_ref, full, send, recv, own_sem):
    spread = Spread(n, x_ref.shape[0], full, send, recv)
    own = pltpu.make_async_copy(x_ref, spread.block(spread.me), own_sem)
    own.start()
    greet(n)
    own.wait()
    spread.start_own(0)

    def body(i, carry):
        pl.when(i + 1 < spread.stages)(lambda: spread.start_own(i + 1))
        spread.start_cross(i)
        return carry

    lax.fori_loop(0, spread.stages, body, 0)

    def arrive(i, carry):
        spread.wait_for(index_of(i // PLANES, i % PLANES, 1 - spread.c))
        return carry

    lax.fori_loop(0, n // CORES, arrive, 0)
    spread.finish()


def gather_rows(n, x):
    rows, width = x.shape
    return pl.pallas_call(
        functools.partial(gather_kernel, n),
        out_shape=jax.ShapeDtypeStruct((n * rows, width), x.dtype),
        in_specs=[pl.BlockSpec(memory_space=pltpu.VMEM)],
        out_specs=pl.BlockSpec(memory_space=pltpu.VMEM),
        scratch_shapes=[
            pltpu.SemaphoreType.DMA((n, 4)),
            pltpu.SemaphoreType.DMA((n,)),
            pltpu.SemaphoreType.DMA,
        ],
        compiler_params=pltpu.CompilerParams(collective_id=0, has_side_effects=True),
    )(x)


def ffn_kernel(
    n,
    x_hbm,
    gate_hbm,
    up_hbm,
    down_hbm,
    out_ref,
    full,
    gate,
    up,
    down,
    part,
    from_core,
    from_plane,
    from_stage,
    send,
    recv,
    core_send,
    core_recv,
    plane_send,
    plane_recv,
    stage_send,
    stage_recv,
    local_sem,
):
    rows = x_hbm.shape[0]
    width = x_hbm.shape[1]
    spread = Spread(n, rows, full, send, recv)
    me, z, y, c = spread.me, spread.z, spread.y, spread.c
    stages = spread.stages
    own = pltpu.make_async_copy(x_hbm, spread.block(me), local_sem.at[0])
    own.start()
    weights = [
        pltpu.make_async_copy(gate_hbm, gate, local_sem.at[1]),
        pltpu.make_async_copy(up_hbm, up, local_sem.at[2]),
        pltpu.make_async_copy(down_hbm, down, local_sem.at[3]),
    ]
    greet(n)
    own.wait()
    spread.start_own(0)
    for copy in weights:
        copy.start()

    def span(b):
        return pl.ds(pl.multiple_of(b * rows, rows), rows)

    def chip_of(k):
        far = near_first(z, k // 2, stages)
        return far, jnp.where(k % 2 == 0, y, 1 - y)

    def core_copy(chip):
        theirs = span(chip * CORES + 1 - c)
        return remote(
            part.at[theirs],
            from_core.at[span(chip)],
            core_send.at[chip],
            core_recv.at[chip],
            index_of(z, y, 1 - c),
        )

    def plane_copy(far):
        return remote(
            part.at[span(index_of(far, 1 - y, c))],
            from_plane.at[span(far)],
            plane_send.at[far],
            plane_recv.at[far],
            index_of(z, 1 - y, c),
        )

    def stage_copy(far, slot, target):
        return remote(
            part.at[span(index_of(far, y, c))],
            from_stage.at[span(slot)],
            stage_send.at[far],
            stage_recv.at[slot],
            target,
        )

    def wide(ref, where):
        return ref[where, :].astype(jnp.float32)

    def join_cores(k):
        far, plane = chip_of(k)
        chip = far * PLANES + plane
        core_copy(chip).wait_recv()
        mine = span(chip * CORES + c)
        part[mine, :] = (wide(part, mine) + wide(from_core, span(chip))).astype(part.dtype)
        pl.when(k % 2 == 1)(lambda: plane_copy(far).start())

    def step(k, carry):
        i = k // 2

        @pl.when(k % 2 == 1)
        def _():
            pl.when(i + 1 < stages)(lambda: spread.start_own(i + 1))
            spread.start_cross(i)

        far, plane = chip_of(k)
        chip = far * PLANES + plane
        spread.wait_for(chip * CORES + 1 - c)

        @pl.when(k == 0)
        def _():
            for copy in weights:
                copy.wait()

        both = pl.ds(pl.multiple_of(chip * CORES * rows, CORES * rows), CORES * rows)
        x = full[both, :]
        gate_out = jnp.dot(x, gate[...], preferred_element_type=jnp.float32)
        up_out = jnp.dot(x, up[...], preferred_element_type=jnp.float32)
        inner = (gate_out / (1.0 + jnp.exp(-gate_out)) * up_out).astype(jnp.bfloat16)
        tile = DOWN_TILE if width % DOWN_TILE == 0 else width
        for at in range(0, width, tile):
            part[both, at : at + tile] = jnp.dot(
                inner, down[:, at : at + tile], preferred_element_type=jnp.float32
            ).astype(part.dtype)
        core_copy(chip).start()
        pl.when(k > 0)(lambda: join_cores(k - 1))
        return carry

    lax.fori_loop(0, PLANES * stages, step, 0)
    join_cores(PLANES * stages - 1)

    def chain(j, carry):
        far = near_first(z, stages - 1 - j, stages)
        down_way = far < z
        slot = jnp.where(down_way, far, far + 1)
        target = index_of(jnp.where(down_way, z - 1, z + 1), y, c)
        fed = jnp.where(down_way, z < stages - 1, z > 0)
        mine = span(index_of(far, y, c))
        plane_copy(far).wait_recv()
        copy = stage_copy(far, slot, target)

        @pl.when(fed)
        def _():
            copy.wait_recv()
            part[mine, :] = (
                wide(part, mine) + wide(from_plane, span(far)) + wide(from_stage, span(slot))
            ).astype(part.dtype)

        @pl.when(jnp.logical_not(fed))
        def _():
            part[mine, :] = (wide(part, mine) + wide(from_plane, span(far))).astype(part.dtype)

        copy.start()
        return carry

    lax.fori_loop(0, stages - 1, chain, 0)

    plane_copy(z).wait_recv()
    mine = span(me)
    out_ref[...] = wide(part, mine) + wide(from_plane, span(z))

    @pl.when(z < stages - 1)
    def _():
        stage_copy(z, z, index_of(z, 1 - y, c)).wait_recv()
        out_ref[...] += wide(from_stage, span(z))

    @pl.when(z > 0)
    def _():
        stage_copy(z, z + 1, index_of(z, 1 - y, c)).wait_recv()
        out_ref[...] += wide(from_stage, span(z + 1))

    def settle(i, carry):
        core_copy(i).wait_send()
        return carry

    lax.fori_loop(0, PLANES * stages, settle, 0)

    def settle_stage(i, carry):
        plane_copy(i).wait_send()
        pl.when(i != z)(lambda: stage_copy(i, i, index_of(z, 1 - y, c)).wait_send())
        return carry

    lax.fori_loop(0, stages, settle_stage, 0)
    spread.finish()


def feed_forward(n, x, gate_weight, up_weight, down_weight):
    rows, width = x.shape
    stages = n // (PLANES * CORES)
    bf16 = jnp.bfloat16
    return pl.pallas_call(
        functools.partial(ffn_kernel, n),
        out_shape=jax.ShapeDtypeStruct((rows, width), jnp.float32),
        in_specs=[pl.BlockSpec(memory_space=pl.ANY)] * 4,
        out_specs=pl.BlockSpec(memory_space=pltpu.VMEM),
        scratch_shapes=[
            pltpu.VMEM((n * rows, width), bf16),
            pltpu.VMEM(gate_weight.shape, bf16),
            pltpu.VMEM(up_weight.shape, bf16),
            pltpu.VMEM(down_weight.shape, bf16),
            pltpu.VMEM((n * rows, width), bf16),
            pltpu.VMEM((n // CORES * rows, width), bf16),
            pltpu.VMEM((stages * rows, width), bf16),
            pltpu.VMEM(((stages + 1) * rows, width), bf16),
            pltpu.SemaphoreType.DMA((n, 4)),
            pltpu.SemaphoreType.DMA((n,)),
            pltpu.SemaphoreType.DMA((n // CORES,)),
            pltpu.SemaphoreType.DMA((n // CORES,)),
            pltpu.SemaphoreType.DMA((stages,)),
            pltpu.SemaphoreType.DMA((stages,)),
            pltpu.SemaphoreType.DMA((stages,)),
            pltpu.SemaphoreType.DMA((stages + 1,)),
            pltpu.SemaphoreType.DMA((4,)),
        ],
        compiler_params=pltpu.CompilerParams(
            collective_id=1, has_side_effects=True, vmem_limit_bytes=64 * 1000 * 1000
        ),
    )(x, gate_weight, up_weight, down_weight)


def on_device(
    hidden_in,
    queries,
    keys,
    values,
    out_weight,
    norm_gain,
    gate_weight,
    up_weight,
    down_weight,
    pair_ids,
    roles,
    send_rows,
    send_counts,
):
    devices = lax.axis_size("ctx")
    my_index = lax.axis_index("ctx")
    tok_rows = hidden_in.shape[0]
    head_dim = keys.shape[1]
    head_count = queries.shape[1] // head_dim
    own_begin = my_index * tok_rows
    query_pos = own_begin + jnp.arange(tok_rows, dtype=jnp.int32)
    query_pair = lax.dynamic_slice_in_dim(pair_ids, own_begin, tok_rows)
    query_role = lax.dynamic_slice_in_dim(roles, own_begin, tok_rows)
    query_heads = queries.reshape(tok_rows, head_count, head_dim)
    score_scale = 1.0 / head_dim**0.5
    both = gather_rows(devices, jnp.concatenate([keys, values], axis=1))
    key_piece, value_piece = both[:, :head_dim], both[:, head_dim:]
    row_count = key_piece.shape[0]
    key_pos = jnp.arange(row_count, dtype=jnp.int32)
    seen_mask = (
        (query_pair[:, None] == pair_ids[None, :])
        & (key_pos[None, :] <= query_pos[:, None])
        & ((roles[None, :] == 0) | (roles[None, :] == query_role[:, None]))
    )
    maximum = jnp.full((head_count, tok_rows), NEG_FILL, jnp.float32)
    scores = (
        jnp.einsum("tqd,kd->qtk", query_heads, key_piece, preferred_element_type=jnp.float32)
        * score_scale
    )
    masked = jnp.where(seen_mask[None], scores, NEG_FILL)
    fresh_max = jnp.maximum(maximum, jnp.max(masked, axis=-1))
    weights = jnp.where(seen_mask[None], jnp.exp(masked - fresh_max[..., None]), 0.0)
    denominator = jnp.sum(weights, axis=-1)
    numerator = jnp.einsum(
        "qtk,kd->qtd", weights.astype(jnp.bfloat16), value_piece, preferred_element_type=jnp.float32
    )
    maximum, denominator, numerator = (fresh_max, denominator, numerator)
    attention = (
        (numerator / denominator[..., None])
        .transpose(1, 0, 2)
        .reshape(tok_rows, head_count * head_dim)
        .astype(jnp.bfloat16)
    )
    residual = (
        hidden_in.astype(jnp.float32)
        + jnp.dot(attention, out_weight, preferred_element_type=jnp.float32)
    ).astype(jnp.bfloat16)
    wide = residual.astype(jnp.float32)
    mean_sq = jnp.mean(wide * wide, axis=-1, keepdims=True)
    normed = (wide * lax.rsqrt(mean_sq + 1e-06) * norm_gain[None, :]).astype(jnp.bfloat16)
    slot_total = send_rows.shape[1]
    capacity = slot_total // devices
    rows_flat = send_rows[0]
    my_counts = lax.dynamic_slice_in_dim(send_counts, my_index, 1, 0)[0]
    valid = jnp.tile(jnp.arange(capacity, dtype=jnp.int32), devices) < jnp.repeat(
        my_counts, capacity
    )
    target = jnp.where(valid, rows_flat, tok_rows)
    summed = feed_forward(devices, normed, gate_weight, up_weight, down_weight)
    live_mask = jnp.zeros((tok_rows,), jnp.float32).at[target].set(1.0, mode="drop")
    ffn_round = lax.optimization_barrier(summed.astype(jnp.bfloat16))
    ffn_back = ffn_round.astype(jnp.float32) * live_mask[:, None]
    return (residual.astype(jnp.float32) + ffn_back).astype(jnp.bfloat16)


def solution(mesh):
    return jax.shard_map(
        on_device,
        mesh=mesh,
        in_specs=(
            P(("groups", "ctx"), None),
            P(("groups", "ctx"), None),
            P(("groups", "ctx"), None),
            P(("groups", "ctx"), None),
            P(),
            P(),
            P(None, "ctx"),
            P(None, "ctx"),
            P("ctx", None),
            P("groups"),
            P("groups"),
            P(("groups", "ctx"), None),
            P("groups", None),
        ),
        out_specs=P(("groups", "ctx"), None),
        check_vma=False,
    )
```

```python
import functools

import jax
import jax.numpy as jnp
from jax import lax
from jax.experimental import pallas as pl
from jax.experimental.pallas import tpu as pltpu
from jax.sharding import PartitionSpec as P

NEG_FILL = -1e30
MESH = pl.DeviceIdType.MESH
PLANES = 2
CORES = 2
DOWN_TILE = 512
PIECES = 2


def place(n):
    me = lax.axis_index("ctx")
    return me, me // (PLANES * CORES), (me // CORES) % PLANES, me % CORES


def index_of(z, y, c):
    return (z * PLANES + y) * CORES + c


def near_first(z, i, stages):
    short = jnp.minimum(z, stages - 1 - z)
    step = (i + 1) // 2
    inner = jnp.where(i % 2 == 1, z + step, z - step)
    outer = jnp.where(z < stages - 1 - z, z + i - short, z - i + short)
    return jnp.where(i <= 2 * short, inner, outer)


def greet(n):
    me, z, y, c = place(n)
    stages = n // (PLANES * CORES)
    barrier = pltpu.get_barrier_semaphore()

    def hello(target):
        pl.semaphore_signal(barrier, inc=1, device_id={"ctx": target}, device_id_type=MESH)

    hello(index_of(z, 1 - y, c))
    hello(index_of(z, y, 1 - c))
    pl.when(z > 0)(lambda: hello(index_of(z - 1, y, c)))
    pl.when(z < stages - 1)(lambda: hello(index_of(z + 1, y, c)))
    pl.semaphore_wait(barrier, 2 + (z > 0).astype(jnp.int32) + (z < stages - 1).astype(jnp.int32))


def remote(src, dst, send_sem, recv_sem, target):
    return pltpu.make_async_remote_copy(
        src_ref=src,
        dst_ref=dst,
        send_sem=send_sem,
        recv_sem=recv_sem,
        device_id={"ctx": target},
        device_id_type=MESH,
    )


class Spread:
    def __init__(self, n, rows, full, send, recv, pieces=1):
        self.pieces, self.piece_rows = pieces, rows // pieces
        self.n, self.rows, self.full, self.send, self.recv = n, rows, full, send, recv
        self.me, self.z, self.y, self.c = place(n)
        self.stages = n // (PLANES * CORES)

    def block(self, b):
        return self.full.at[pl.ds(pl.multiple_of(b * self.rows, self.rows), self.rows)]

    def copy(self, b, way, target, p):
        begin = pl.multiple_of(b * self.rows + p * self.piece_rows, self.piece_rows)
        piece = self.full.at[pl.ds(begin, self.piece_rows)]
        return remote(piece, piece, self.send.at[b, way, p], self.recv.at[b, p], target)

    def wait_piece(self, b, p):
        self.copy(b, 0, index_of(self.z, self.y, 1 - self.c), p).wait_recv()

    def wait_for(self, b):
        for p in range(self.pieces):
            self.wait_piece(b, p)

    def ways(self, i, p, act):
        z, y, c = self.z, self.y, self.c
        far = near_first(z, i, self.stages)
        b = index_of(far, y, c)
        act(self.copy(b, 0, index_of(z, 1 - y, c), p))
        pl.when((z < self.stages - 1) & (far <= z))(
            lambda: act(self.copy(b, 1, index_of(z + 1, y, c), p))
        )
        pl.when((z > 0) & (far >= z))(lambda: act(self.copy(b, 2, index_of(z - 1, y, c), p)))
        act(self.copy(b, 3, index_of(z, y, 1 - c), p))

    def start_own(self, i):
        b = index_of(near_first(self.z, i, self.stages), self.y, self.c)
        for p in range(self.pieces):
            pl.when(i > 0)(functools.partial(self.wait_piece, b, p))
            self.ways(i, p, lambda copy: copy.start())

    def cross(self, i, p):
        b = index_of(near_first(self.z, i, self.stages), 1 - self.y, self.c)
        return b, self.copy(b, 3, index_of(self.z, self.y, 1 - self.c), p)

    def start_cross(self, i):
        for p in range(self.pieces):
            b, copy = self.cross(i, p)
            self.wait_piece(b, p)
            copy.start()

    def finish(self):
        def body(i, carry):
            for p in range(self.pieces):
                self.ways(i, p, lambda copy: copy.wait_send())
                self.cross(i, p)[1].wait_send()
            return carry

        lax.fori_loop(0, self.stages, body, 0)


def gather_kernel(n, x_ref, full, send, recv, own_sem):
    spread = Spread(n, x_ref.shape[0], full, send, recv)
    own = pltpu.make_async_copy(x_ref, spread.block(spread.me), own_sem)
    own.start()
    greet(n)
    own.wait()
    spread.start_own(0)

    def body(i, carry):
        pl.when(i + 1 < spread.stages)(lambda: spread.start_own(i + 1))
        spread.start_cross(i)
        return carry

    lax.fori_loop(0, spread.stages, body, 0)

    def arrive(i, carry):
        spread.wait_for(index_of(i // PLANES, i % PLANES, 1 - spread.c))
        return carry

    lax.fori_loop(0, n // CORES, arrive, 0)
    spread.finish()


def gather_rows(n, x):
    rows, width = x.shape
    return pl.pallas_call(
        functools.partial(gather_kernel, n),
        out_shape=jax.ShapeDtypeStruct((n * rows, width), x.dtype),
        in_specs=[pl.BlockSpec(memory_space=pltpu.VMEM)],
        out_specs=pl.BlockSpec(memory_space=pltpu.VMEM),
        scratch_shapes=[
            pltpu.SemaphoreType.DMA((n, 4, 1)),
            pltpu.SemaphoreType.DMA((n, 1)),
            pltpu.SemaphoreType.DMA,
        ],
        compiler_params=pltpu.CompilerParams(collective_id=0, has_side_effects=True),
    )(x)


def ffn_kernel(
    n,
    x_hbm,
    gate_hbm,
    up_hbm,
    down_hbm,
    out_ref,
    full,
    gate,
    up,
    down,
    part,
    from_core,
    from_plane,
    from_stage,
    send,
    recv,
    core_send,
    core_recv,
    plane_send,
    plane_recv,
    stage_send,
    stage_recv,
    local_sem,
):
    rows = x_hbm.shape[0]
    width = x_hbm.shape[1]
    spread = Spread(n, rows, full, send, recv, PIECES)
    me, z, y, c = spread.me, spread.z, spread.y, spread.c
    stages = spread.stages
    own = pltpu.make_async_copy(x_hbm, spread.block(me), local_sem.at[0])
    own.start()
    weights = [
        pltpu.make_async_copy(gate_hbm, gate, local_sem.at[1]),
        pltpu.make_async_copy(up_hbm, up, local_sem.at[2]),
        pltpu.make_async_copy(down_hbm, down, local_sem.at[3]),
    ]
    greet(n)
    own.wait()
    spread.start_own(0)
    for copy in weights:
        copy.start()

    def span(b):
        return pl.ds(pl.multiple_of(b * rows, rows), rows)

    def chip_of(k):
        far = near_first(z, k // 2, stages)
        return far, jnp.where(k % 2 == 0, y, 1 - y)

    def core_copy(chip):
        theirs = span(chip * CORES + 1 - c)
        return remote(
            part.at[theirs],
            from_core.at[span(chip)],
            core_send.at[chip],
            core_recv.at[chip],
            index_of(z, y, 1 - c),
        )

    def plane_copy(far):
        return remote(
            part.at[span(index_of(far, 1 - y, c))],
            from_plane.at[span(far)],
            plane_send.at[far],
            plane_recv.at[far],
            index_of(z, 1 - y, c),
        )

    piece_rows = rows // PIECES

    def piece(b, p):
        return pl.ds(pl.multiple_of(b * rows + p * piece_rows, piece_rows), piece_rows)

    def stage_copy(far, slot, target, p):
        return remote(
            part.at[piece(index_of(far, y, c), p)],
            from_stage.at[piece(slot, p)],
            stage_send.at[far, p],
            stage_recv.at[slot, p],
            target,
        )

    def wide(ref, where):
        return ref[where, :].astype(jnp.float32)

    def join_cores(k):
        far, plane = chip_of(k)
        chip = far * PLANES + plane
        core_copy(chip).wait_recv()
        mine = span(chip * CORES + c)
        part[mine, :] = (wide(part, mine) + wide(from_core, span(chip))).astype(part.dtype)
        pl.when(k % 2 == 1)(lambda: plane_copy(far).start())

    def step(k, carry):
        i = k // 2

        @pl.when(k % 2 == 1)
        def _():
            pl.when(i + 1 < stages)(lambda: spread.start_own(i + 1))
            spread.start_cross(i)

        far, plane = chip_of(k)
        chip = far * PLANES + plane
        spread.wait_for(chip * CORES + 1 - c)

        @pl.when(k == 0)
        def _():
            for copy in weights:
                copy.wait()

        both = pl.ds(pl.multiple_of(chip * CORES * rows, CORES * rows), CORES * rows)
        x = full[both, :]
        turned = (((1,), (1,)), ((), ()))
        gate_out = lax.dot_general(x, gate[...], turned, preferred_element_type=jnp.float32)
        up_out = lax.dot_general(x, up[...], turned, preferred_element_type=jnp.float32)
        inner = (gate_out / (1.0 + jnp.exp(-gate_out)) * up_out).astype(jnp.bfloat16)
        tile = DOWN_TILE if width % DOWN_TILE == 0 else width
        for at in range(0, width, tile):
            part[both, at : at + tile] = jnp.dot(
                inner, down[:, at : at + tile], preferred_element_type=jnp.float32
            ).astype(part.dtype)
        core_copy(chip).start()
        pl.when(k > 0)(lambda: join_cores(k - 1))
        return carry

    lax.fori_loop(0, PLANES * stages, step, 0)
    join_cores(PLANES * stages - 1)

    def add_piece(fed, copy, mine, across, along):
        @pl.when(fed)
        def _():
            copy.wait_recv()
            part[mine, :] = (
                wide(part, mine) + wide(from_plane, across) + wide(from_stage, along)
            ).astype(part.dtype)

        @pl.when(jnp.logical_not(fed))
        def _():
            part[mine, :] = (wide(part, mine) + wide(from_plane, across)).astype(part.dtype)

    def chain(j, carry):
        far = near_first(z, stages - 1 - j, stages)
        down_way = far < z
        slot = jnp.where(down_way, far, far + 1)
        target = index_of(jnp.where(down_way, z - 1, z + 1), y, c)
        fed = jnp.where(down_way, z < stages - 1, z > 0)
        plane_copy(far).wait_recv()
        for p in range(PIECES):
            mine = piece(index_of(far, y, c), p)
            copy = stage_copy(far, slot, target, p)
            add_piece(fed, copy, mine, piece(far, p), piece(slot, p))
            copy.start()
        return carry

    lax.fori_loop(0, stages - 1, chain, 0)

    plane_copy(z).wait_recv()
    mine = span(me)
    out_ref[...] = wide(part, mine) + wide(from_plane, span(z))

    @pl.when(z < stages - 1)
    def _():
        for p in range(PIECES):
            stage_copy(z, z, index_of(z, 1 - y, c), p).wait_recv()
        out_ref[...] += wide(from_stage, span(z))

    @pl.when(z > 0)
    def _():
        for p in range(PIECES):
            stage_copy(z, z + 1, index_of(z, 1 - y, c), p).wait_recv()
        out_ref[...] += wide(from_stage, span(z + 1))

    def settle(i, carry):
        core_copy(i).wait_send()
        return carry

    lax.fori_loop(0, PLANES * stages, settle, 0)

    def settle_stage(i, carry):
        plane_copy(i).wait_send()
        for p in range(PIECES):
            stage = stage_copy(i, i, index_of(z, 1 - y, c), p)
            pl.when(i != z)(stage.wait_send)
        return carry

    lax.fori_loop(0, stages, settle_stage, 0)
    spread.finish()


def feed_forward(n, x, gate_weight, up_weight, down_weight):
    rows, width = x.shape
    stages = n // (PLANES * CORES)
    bf16 = jnp.bfloat16
    return pl.pallas_call(
        functools.partial(ffn_kernel, n),
        out_shape=jax.ShapeDtypeStruct((rows, width), jnp.float32),
        in_specs=[pl.BlockSpec(memory_space=pl.ANY)] * 4,
        out_specs=pl.BlockSpec(memory_space=pltpu.VMEM),
        scratch_shapes=[
            pltpu.VMEM((n * rows, width), bf16),
            pltpu.VMEM(gate_weight.shape, bf16),
            pltpu.VMEM(up_weight.shape, bf16),
            pltpu.VMEM(down_weight.shape, bf16),
            pltpu.VMEM((n * rows, width), bf16),
            pltpu.VMEM((n // CORES * rows, width), bf16),
            pltpu.VMEM((stages * rows, width), bf16),
            pltpu.VMEM(((stages + 1) * rows, width), bf16),
            pltpu.SemaphoreType.DMA((n, 4, PIECES)),
            pltpu.SemaphoreType.DMA((n, PIECES)),
            pltpu.SemaphoreType.DMA((n // CORES,)),
            pltpu.SemaphoreType.DMA((n // CORES,)),
            pltpu.SemaphoreType.DMA((stages,)),
            pltpu.SemaphoreType.DMA((stages,)),
            pltpu.SemaphoreType.DMA((stages, PIECES)),
            pltpu.SemaphoreType.DMA((stages + 1, PIECES)),
            pltpu.SemaphoreType.DMA((4,)),
        ],
        compiler_params=pltpu.CompilerParams(
            collective_id=1, has_side_effects=True, vmem_limit_bytes=64 * 1000 * 1000
        ),
    )(x, gate_weight, up_weight, down_weight)


def on_device(
    hidden_in,
    queries,
    keys,
    values,
    out_weight,
    norm_gain,
    gate_weight,
    up_weight,
    down_weight,
    pair_ids,
    roles,
    send_rows,
    send_counts,
):
    devices = lax.axis_size("ctx")
    my_index = lax.axis_index("ctx")
    tok_rows = hidden_in.shape[0]
    head_dim = keys.shape[1]
    head_count = queries.shape[1] // head_dim
    own_begin = my_index * tok_rows
    query_pos = own_begin + jnp.arange(tok_rows, dtype=jnp.int32)
    query_pair = lax.dynamic_slice_in_dim(pair_ids, own_begin, tok_rows)
    query_role = lax.dynamic_slice_in_dim(roles, own_begin, tok_rows)
    query_heads = queries.reshape(tok_rows, head_count, head_dim)
    score_scale = 1.0 / head_dim**0.5
    both = gather_rows(devices, jnp.concatenate([keys, values], axis=1))
    key_piece, value_piece = both[:, :head_dim], both[:, head_dim:]
    row_count = key_piece.shape[0]
    key_pos = jnp.arange(row_count, dtype=jnp.int32)
    seen_mask = (
        (query_pair[:, None] == pair_ids[None, :])
        & (key_pos[None, :] <= query_pos[:, None])
        & ((roles[None, :] == 0) | (roles[None, :] == query_role[:, None]))
    )
    maximum = jnp.full((head_count, tok_rows), NEG_FILL, jnp.float32)
    scores = (
        jnp.einsum("tqd,kd->qtk", query_heads, key_piece, preferred_element_type=jnp.float32)
        * score_scale
    )
    masked = jnp.where(seen_mask[None], scores, NEG_FILL)
    fresh_max = jnp.maximum(maximum, jnp.max(masked, axis=-1))
    weights = jnp.where(seen_mask[None], jnp.exp(masked - fresh_max[..., None]), 0.0)
    denominator = jnp.sum(weights, axis=-1)
    numerator = jnp.einsum(
        "qtk,kd->qtd", weights.astype(jnp.bfloat16), value_piece, preferred_element_type=jnp.float32
    )
    maximum, denominator, numerator = (fresh_max, denominator, numerator)
    attention = (
        (numerator / denominator[..., None])
        .transpose(1, 0, 2)
        .reshape(tok_rows, head_count * head_dim)
        .astype(jnp.bfloat16)
    )
    residual = (
        hidden_in.astype(jnp.float32)
        + jnp.dot(attention, out_weight, preferred_element_type=jnp.float32)
    ).astype(jnp.bfloat16)
    wide = residual.astype(jnp.float32)
    mean_sq = jnp.mean(wide * wide, axis=-1, keepdims=True)
    normed = (wide * lax.rsqrt(mean_sq + 1e-06) * norm_gain[None, :]).astype(jnp.bfloat16)
    slot_total = send_rows.shape[1]
    capacity = slot_total // devices
    rows_flat = send_rows[0]
    my_counts = lax.dynamic_slice_in_dim(send_counts, my_index, 1, 0)[0]
    valid = jnp.tile(jnp.arange(capacity, dtype=jnp.int32), devices) < jnp.repeat(
        my_counts, capacity
    )
    target = jnp.where(valid, rows_flat, tok_rows)
    summed = feed_forward(devices, normed, gate_weight.T, up_weight.T, down_weight)
    live_mask = jnp.zeros((tok_rows,), jnp.float32).at[target].set(1.0, mode="drop")
    ffn_round = lax.optimization_barrier(summed.astype(jnp.bfloat16))
    ffn_back = ffn_round.astype(jnp.float32) * live_mask[:, None]
    return (residual.astype(jnp.float32) + ffn_back).astype(jnp.bfloat16)


def solution(mesh):
    return jax.shard_map(
        on_device,
        mesh=mesh,
        in_specs=(
            P(("groups", "ctx"), None),
            P(("groups", "ctx"), None),
            P(("groups", "ctx"), None),
            P(("groups", "ctx"), None),
            P(),
            P(),
            P(None, "ctx"),
            P(None, "ctx"),
            P("ctx", None),
            P("groups"),
            P("groups"),
            P(("groups", "ctx"), None),
            P("groups", None),
        ),
        out_specs=P(("groups", "ctx"), None),
        check_vma=False,
    )
```

```python
import functools

import jax
import jax.numpy as jnp
from jax import lax
from jax.experimental import pallas as pl
from jax.experimental.pallas import tpu as pltpu
from jax.sharding import PartitionSpec as P

NEG_FILL = -1e30
MESH = pl.DeviceIdType.MESH
PLANES = 2
CORES = 2
DOWN_TILE = 512
PIECES = 2


def place(n):
    me = lax.axis_index("ctx")
    return me, me // (PLANES * CORES), (me // CORES) % PLANES, me % CORES


def index_of(z, y, c):
    return (z * PLANES + y) * CORES + c


def near_first(z, i, stages):
    short = jnp.minimum(z, stages - 1 - z)
    step = (i + 1) // 2
    inner = jnp.where(i % 2 == 1, z + step, z - step)
    outer = jnp.where(z < stages - 1 - z, z + i - short, z - i + short)
    return jnp.where(i <= 2 * short, inner, outer)


def greet(n):
    me, z, y, c = place(n)
    stages = n // (PLANES * CORES)
    barrier = pltpu.get_barrier_semaphore()

    def hello(target):
        pl.semaphore_signal(barrier, inc=1, device_id={"ctx": target}, device_id_type=MESH)

    hello(index_of(z, 1 - y, c))
    hello(index_of(z, y, 1 - c))
    pl.when(z > 0)(lambda: hello(index_of(z - 1, y, c)))
    pl.when(z < stages - 1)(lambda: hello(index_of(z + 1, y, c)))
    pl.semaphore_wait(barrier, 2 + (z > 0).astype(jnp.int32) + (z < stages - 1).astype(jnp.int32))


def remote(src, dst, send_sem, recv_sem, target):
    return pltpu.make_async_remote_copy(
        src_ref=src,
        dst_ref=dst,
        send_sem=send_sem,
        recv_sem=recv_sem,
        device_id={"ctx": target},
        device_id_type=MESH,
    )


class Spread:
    def __init__(self, n, rows, full, send, recv, pieces=1):
        self.pieces, self.piece_rows = pieces, rows // pieces
        self.n, self.rows, self.full, self.send, self.recv = n, rows, full, send, recv
        self.me, self.z, self.y, self.c = place(n)
        self.stages = n // (PLANES * CORES)

    def block(self, b):
        return self.full.at[pl.ds(pl.multiple_of(b * self.rows, self.rows), self.rows)]

    def copy(self, b, way, target, p):
        begin = pl.multiple_of(b * self.rows + p * self.piece_rows, self.piece_rows)
        piece = self.full.at[pl.ds(begin, self.piece_rows)]
        return remote(piece, piece, self.send.at[b, way, p], self.recv.at[b, p], target)

    def wait_piece(self, b, p):
        self.copy(b, 0, index_of(self.z, self.y, 1 - self.c), p).wait_recv()

    def wait_for(self, b):
        for p in range(self.pieces):
            self.wait_piece(b, p)

    def ways(self, i, p, act):
        z, y, c = self.z, self.y, self.c
        far = near_first(z, i, self.stages)
        b = index_of(far, y, c)
        act(self.copy(b, 0, index_of(z, 1 - y, c), p))
        pl.when((z < self.stages - 1) & (far <= z))(
            lambda: act(self.copy(b, 1, index_of(z + 1, y, c), p))
        )
        pl.when((z > 0) & (far >= z))(lambda: act(self.copy(b, 2, index_of(z - 1, y, c), p)))
        act(self.copy(b, 3, index_of(z, y, 1 - c), p))

    def start_own(self, i):
        b = index_of(near_first(self.z, i, self.stages), self.y, self.c)
        for p in range(self.pieces):
            pl.when(i > 0)(functools.partial(self.wait_piece, b, p))
            self.ways(i, p, lambda copy: copy.start())

    def cross(self, i, p):
        b = index_of(near_first(self.z, i, self.stages), 1 - self.y, self.c)
        return b, self.copy(b, 3, index_of(self.z, self.y, 1 - self.c), p)

    def start_cross(self, i):
        for p in range(self.pieces):
            b, copy = self.cross(i, p)
            self.wait_piece(b, p)
            copy.start()

    def finish(self):
        def body(i, carry):
            for p in range(self.pieces):
                self.ways(i, p, lambda copy: copy.wait_send())
                self.cross(i, p)[1].wait_send()
            return carry

        lax.fori_loop(0, self.stages, body, 0)


def gather_kernel(n, x_ref, full, send, recv, own_sem):
    spread = Spread(n, x_ref.shape[0], full, send, recv)
    own = pltpu.make_async_copy(x_ref, spread.block(spread.me), own_sem)
    own.start()
    greet(n)
    own.wait()
    spread.start_own(0)

    def body(i, carry):
        pl.when(i + 1 < spread.stages)(lambda: spread.start_own(i + 1))
        spread.start_cross(i)
        return carry

    lax.fori_loop(0, spread.stages, body, 0)

    def arrive(i, carry):
        spread.wait_for(index_of(i // PLANES, i % PLANES, 1 - spread.c))
        return carry

    lax.fori_loop(0, n // CORES, arrive, 0)
    spread.finish()


def gather_rows(n, x):
    rows, width = x.shape
    return pl.pallas_call(
        functools.partial(gather_kernel, n),
        out_shape=jax.ShapeDtypeStruct((n * rows, width), x.dtype),
        in_specs=[pl.BlockSpec(memory_space=pltpu.VMEM)],
        out_specs=pl.BlockSpec(memory_space=pltpu.VMEM),
        scratch_shapes=[
            pltpu.SemaphoreType.DMA((n, 4, 1)),
            pltpu.SemaphoreType.DMA((n, 1)),
            pltpu.SemaphoreType.DMA,
        ],
        compiler_params=pltpu.CompilerParams(collective_id=0, has_side_effects=True),
    )(x)


def ffn_kernel(
    n,
    x_hbm,
    gate_hbm,
    up_hbm,
    down_hbm,
    out_ref,
    full,
    gate,
    up,
    down,
    part,
    from_core,
    from_plane,
    from_stage,
    from_other,
    send,
    recv,
    core_send,
    core_recv,
    plane_send,
    plane_recv,
    stage_send,
    stage_recv,
    local_sem,
):
    rows = x_hbm.shape[0]
    width = x_hbm.shape[1]
    spread = Spread(n, rows, full, send, recv, PIECES)
    me, z, y, c = spread.me, spread.z, spread.y, spread.c
    stages = spread.stages
    own = pltpu.make_async_copy(x_hbm, spread.block(me), local_sem.at[0])
    own.start()
    weights = [
        pltpu.make_async_copy(gate_hbm, gate, local_sem.at[1]),
        pltpu.make_async_copy(up_hbm, up, local_sem.at[2]),
        pltpu.make_async_copy(down_hbm, down, local_sem.at[3]),
    ]
    greet(n)
    own.wait()
    spread.start_own(0)
    for copy in weights:
        copy.start()

    def span(b):
        return pl.ds(pl.multiple_of(b * rows, rows), rows)

    def chip_of(k):
        far = near_first(z, k // 2, stages)
        return far, jnp.where(k % 2 == 0, y, 1 - y)

    def core_copy(chip):
        theirs = span(chip * CORES + 1 - c)
        return remote(
            part.at[theirs],
            from_core.at[span(chip)],
            core_send.at[chip],
            core_recv.at[chip],
            index_of(z, y, 1 - c),
        )

    piece_rows = rows // PIECES

    def piece(b, p):
        return pl.ds(pl.multiple_of(b * rows + p * piece_rows, piece_rows), piece_rows)

    def plane_copy(far, p=0):
        slot = far if p == 0 else stages
        return remote(
            part.at[piece(index_of(far, 1 - y, c), p)],
            from_plane.at[piece(far, p)],
            plane_send.at[slot],
            plane_recv.at[slot],
            index_of(z, 1 - y, c),
        )

    def sent(far, q):
        return piece(index_of(far, 1 - y if q == 2 else y, c), min(q, 1))

    def landed(slot, q):
        if q == 2:
            return from_other, pl.ds(pl.multiple_of(slot * piece_rows, piece_rows), piece_rows)
        return from_stage, piece(slot, q)

    def stage_copy(far, slot, target, q):
        ref, where = landed(slot, q)
        return remote(
            part.at[sent(far, q)], ref.at[where], stage_send.at[far, q], stage_recv.at[slot, q], target
        )

    def wide(ref, where):
        return ref[where, :].astype(jnp.float32)

    def join_cores(k):
        far, plane = chip_of(k)
        chip = far * PLANES + plane
        core_copy(chip).wait_recv()
        mine = span(chip * CORES + c)
        part[mine, :] = (wide(part, mine) + wide(from_core, span(chip))).astype(part.dtype)
        pl.when(k % 2 == 1)(lambda: plane_copy(far).start())

    def step(k, carry):
        i = k // 2

        @pl.when(k % 2 == 1)
        def _():
            pl.when(i + 1 < stages)(lambda: spread.start_own(i + 1))
            spread.start_cross(i)

        far, plane = chip_of(k)
        chip = far * PLANES + plane
        spread.wait_for(chip * CORES + 1 - c)

        @pl.when(k == 0)
        def _():
            for copy in weights:
                copy.wait()

        both = pl.ds(pl.multiple_of(chip * CORES * rows, CORES * rows), CORES * rows)
        x = full[both, :]
        turned = (((1,), (1,)), ((), ()))
        gate_out = lax.dot_general(x, gate[...], turned, preferred_element_type=jnp.float32)
        up_out = lax.dot_general(x, up[...], turned, preferred_element_type=jnp.float32)
        inner = (gate_out / (1.0 + jnp.exp(-gate_out)) * up_out).astype(jnp.bfloat16)
        tile = DOWN_TILE if width % DOWN_TILE == 0 else width
        for at in range(0, width, tile):
            part[both, at : at + tile] = jnp.dot(
                inner, down[:, at : at + tile], preferred_element_type=jnp.float32
            ).astype(part.dtype)
        core_copy(chip).start()
        pl.when(k > 0)(lambda: join_cores(k - 1))
        return carry

    lax.fori_loop(0, PLANES * stages, step, 0)
    join_cores(PLANES * stages - 1)

    def add(mine, ref, where):
        part[mine, :] = (wide(part, mine) + wide(ref, where)).astype(part.dtype)

    def add_piece(fed, copy, far, slot, q):
        mine = sent(far, q)
        if q == 0:
            plane_copy(far).wait_recv()
            add(mine, from_plane, piece(far, 0))

        @pl.when(fed)
        def _():
            copy.wait_recv()
            add(mine, *landed(slot, q))

    def chain(j, carry):
        far = near_first(z, stages - 1 - j, stages)
        down_way = far < z
        slot = jnp.where(down_way, far, far + 1)
        target = index_of(jnp.where(down_way, z - 1, z + 1), y, c)
        fed = jnp.where(down_way, z < stages - 1, z > 0)
        for q in (2, 1, 0):
            copy = stage_copy(far, slot, target, q)
            add_piece(fed, copy, far, slot, q)
            copy.start()
        return carry

    lax.fori_loop(0, stages - 1, chain, 0)

    for slot, there in ((z, z < stages - 1), (z + 1, z > 0)):
        add_piece(there, stage_copy(z, slot, index_of(z, 1 - y, c), 2), z, slot, 2)
    plane_copy(z, 1).start()
    plane_copy(z).wait_recv()
    plane_copy(z, 1).wait_recv()
    mine = span(me)
    out_ref[...] = wide(part, mine) + wide(from_plane, span(z))

    @pl.when(z < stages - 1)
    def _():
        for p in range(PIECES):
            stage_copy(z, z, index_of(z, 1 - y, c), p).wait_recv()
        out_ref[...] += wide(from_stage, span(z))

    @pl.when(z > 0)
    def _():
        for p in range(PIECES):
            stage_copy(z, z + 1, index_of(z, 1 - y, c), p).wait_recv()
        out_ref[...] += wide(from_stage, span(z + 1))

    def settle(i, carry):
        core_copy(i).wait_send()
        return carry

    lax.fori_loop(0, PLANES * stages, settle, 0)

    def settle_stage(i, carry):
        plane_copy(i).wait_send()
        for q in range(3):
            stage = stage_copy(i, i, index_of(z, 1 - y, c), q)
            pl.when(i != z)(stage.wait_send)
        return carry

    lax.fori_loop(0, stages, settle_stage, 0)
    plane_copy(z, 1).wait_send()
    spread.finish()


def feed_forward(n, x, gate_weight, up_weight, down_weight):
    rows, width = x.shape
    stages = n // (PLANES * CORES)
    bf16 = jnp.bfloat16
    return pl.pallas_call(
        functools.partial(ffn_kernel, n),
        out_shape=jax.ShapeDtypeStruct((rows, width), jnp.float32),
        in_specs=[pl.BlockSpec(memory_space=pl.ANY)] * 4,
        out_specs=pl.BlockSpec(memory_space=pltpu.VMEM),
        scratch_shapes=[
            pltpu.VMEM((n * rows, width), bf16),
            pltpu.VMEM(gate_weight.shape, bf16),
            pltpu.VMEM(up_weight.shape, bf16),
            pltpu.VMEM(down_weight.shape, bf16),
            pltpu.VMEM((n * rows, width), bf16),
            pltpu.VMEM((n // CORES * rows, width), bf16),
            pltpu.VMEM((stages * rows, width), bf16),
            pltpu.VMEM(((stages + 1) * rows, width), bf16),
            pltpu.VMEM(((stages + 1) * (rows // PIECES), width), bf16),
            pltpu.SemaphoreType.DMA((n, 4, PIECES)),
            pltpu.SemaphoreType.DMA((n, PIECES)),
            pltpu.SemaphoreType.DMA((n // CORES,)),
            pltpu.SemaphoreType.DMA((n // CORES,)),
            pltpu.SemaphoreType.DMA((stages + 1,)),
            pltpu.SemaphoreType.DMA((stages + 1,)),
            pltpu.SemaphoreType.DMA((stages, 3)),
            pltpu.SemaphoreType.DMA((stages + 1, 3)),
            pltpu.SemaphoreType.DMA((4,)),
        ],
        compiler_params=pltpu.CompilerParams(
            collective_id=1, has_side_effects=True, vmem_limit_bytes=64 * 1000 * 1000
        ),
    )(x, gate_weight, up_weight, down_weight)


def on_device(
    hidden_in,
    queries,
    keys,
    values,
    out_weight,
    norm_gain,
    gate_weight,
    up_weight,
    down_weight,
    pair_ids,
    roles,
    send_rows,
    send_counts,
):
    devices = lax.axis_size("ctx")
    my_index = lax.axis_index("ctx")
    tok_rows = hidden_in.shape[0]
    head_dim = keys.shape[1]
    head_count = queries.shape[1] // head_dim
    own_begin = my_index * tok_rows
    query_pos = own_begin + jnp.arange(tok_rows, dtype=jnp.int32)
    query_pair = lax.dynamic_slice_in_dim(pair_ids, own_begin, tok_rows)
    query_role = lax.dynamic_slice_in_dim(roles, own_begin, tok_rows)
    query_heads = queries.reshape(tok_rows, head_count, head_dim)
    score_scale = 1.0 / head_dim**0.5
    both = gather_rows(devices, jnp.concatenate([keys, values], axis=1))
    key_piece, value_piece = both[:, :head_dim], both[:, head_dim:]
    row_count = key_piece.shape[0]
    key_pos = jnp.arange(row_count, dtype=jnp.int32)
    seen_mask = (
        (query_pair[:, None] == pair_ids[None, :])
        & (key_pos[None, :] <= query_pos[:, None])
        & ((roles[None, :] == 0) | (roles[None, :] == query_role[:, None]))
    )
    maximum = jnp.full((head_count, tok_rows), NEG_FILL, jnp.float32)
    scores = (
        jnp.einsum("tqd,kd->qtk", query_heads, key_piece, preferred_element_type=jnp.float32)
        * score_scale
    )
    masked = jnp.where(seen_mask[None], scores, NEG_FILL)
    fresh_max = jnp.maximum(maximum, jnp.max(masked, axis=-1))
    weights = jnp.where(seen_mask[None], jnp.exp(masked - fresh_max[..., None]), 0.0)
    denominator = jnp.sum(weights, axis=-1)
    numerator = jnp.einsum(
        "qtk,kd->qtd", weights.astype(jnp.bfloat16), value_piece, preferred_element_type=jnp.float32
    )
    maximum, denominator, numerator = (fresh_max, denominator, numerator)
    attention = (
        (numerator / denominator[..., None])
        .transpose(1, 0, 2)
        .reshape(tok_rows, head_count * head_dim)
        .astype(jnp.bfloat16)
    )
    residual = (
        hidden_in.astype(jnp.float32)
        + jnp.dot(attention, out_weight, preferred_element_type=jnp.float32)
    ).astype(jnp.bfloat16)
    wide = residual.astype(jnp.float32)
    mean_sq = jnp.mean(wide * wide, axis=-1, keepdims=True)
    normed = (wide * lax.rsqrt(mean_sq + 1e-06) * norm_gain[None, :]).astype(jnp.bfloat16)
    slot_total = send_rows.shape[1]
    capacity = slot_total // devices
    rows_flat = send_rows[0]
    my_counts = lax.dynamic_slice_in_dim(send_counts, my_index, 1, 0)[0]
    valid = jnp.tile(jnp.arange(capacity, dtype=jnp.int32), devices) < jnp.repeat(
        my_counts, capacity
    )
    target = jnp.where(valid, rows_flat, tok_rows)
    summed = feed_forward(devices, normed, gate_weight.T, up_weight.T, down_weight)
    live_mask = jnp.zeros((tok_rows,), jnp.float32).at[target].set(1.0, mode="drop")
    ffn_round = lax.optimization_barrier(summed.astype(jnp.bfloat16))
    ffn_back = ffn_round.astype(jnp.float32) * live_mask[:, None]
    return (residual.astype(jnp.float32) + ffn_back).astype(jnp.bfloat16)


def solution(mesh):
    return jax.shard_map(
        on_device,
        mesh=mesh,
        in_specs=(
            P(("groups", "ctx"), None),
            P(("groups", "ctx"), None),
            P(("groups", "ctx"), None),
            P(("groups", "ctx"), None),
            P(),
            P(),
            P(None, "ctx"),
            P(None, "ctx"),
            P("ctx", None),
            P("groups"),
            P("groups"),
            P(("groups", "ctx"), None),
            P("groups", None),
        ),
        out_specs=P(("groups", "ctx"), None),
        check_vma=False,
    )
```
